32 devices in a mesh: ep: 16 (over z, y, core), rep: 2 (over x).
Axes of the slice: x: 2, y: 2, z: 4, core: 2. Of those that a mesh axis runs over, the one named last changes fastest.
Arguments:
- out_grad: bfloat16 [4096, 2048], P(('ep', 'rep')), may hold values from -6 to 6
- hidden: bfloat16 [4096, 8, 768], P(('ep', 'rep')), may hold values from -6 to 6
- expert_ids: int32 [4096, 8], P(('ep', 'rep')), may hold values from 0 to 15, all different within a row; in each aligned block of 128 rows (0 to 127, 128 to 255, ...) at most 72 rows name the same one
- gates: float32 [4096, 8], P(('ep', 'rep')), may hold values from 0.02 to 0.5
- weights: bfloat16 [16, 768, 2048], P('ep', 'rep'), may hold values from -0.125 to 0.125
- row_moment: float32 [16, 768], P('ep', 'rep'), may hold values from 16 to 1024
- col_moment: float32 [16, 2, 2048], P('ep', 'rep'), may hold values from 16 to 1024
Outputs:
- hidden_grad: bfloat16 [4096, 8, 768], P(('ep', 'rep'))
- update: bfloat16 [16, 768, 2048], P('ep', 'rep')
- row_new: float32 [16, 768], P('ep', 'rep')
- col_new: float32 [16, 2, 2048], P('ep', 'rep')
The draws below stay inside these ranges and needn't reach their ends.
Inputs may be any that keep to these rules, and one draw needn't show every extreme that they name: `expert_ids`: the 8 experts of a token are distinct. Among the tokens of one device no expert is chosen more than 72 times, and in every draw some device reaches 72 for some expert.
All inputs are finite; a program needn't handle non-finite values.
Results may differ from the reference program's by a relative error of at most 0.014.
Values may be sent and summed in bfloat16 or wider, within the bound.
A program may use at most 128 MiB of HBM per device.

```python
import math
import jax
import jax.numpy as jnp
import numpy as np
from jax import lax

D = 2048
FF = 768
TOP = 8
TOK_DEV = 128
EXPERTS = 16
CAP = 72
BLK = 384
TOKENS = 4096
N_EP = 16
N_REP = 2


def block_levels(stream_key, extent, cuts, smallest, largest):
    loudness = 1.0
    for position, parts in cuts:
        steps = jax.random.uniform(jax.random.fold_in(jax.random.fold_in(stream_key, 6), position), (parts,), jnp.float32, smallest / len(cuts), largest / len(cuts))
        loudness = loudness * jnp.repeat(jnp.exp(steps), extent[position] // parts).reshape((-1,) + (1,) * (len(extent) - 1 - position))
    return loudness


def routed_block(rng, own, number, rows, number_of, top, bound, lean):
    ranking = jax.random.permutation(rng, number_of)
    packed, usual = portions_of(number_of, rows * top, bound, lean, True), portions_of(number_of, rows * top, bound, lean, False)
    places = jnp.arange(number_of)

    def named(sizes, offset_by):
        used = int((sizes > 0).sum())
        fixed = max(1, used // 4)
        shifted = fixed + (places - fixed + offset_by * (used - fixed)) % max(1, number_of - fixed)
        return jnp.zeros((number_of,), jnp.int32).at[ranking[jnp.where(places < fixed, places, shifted)]].set(jnp.asarray(sizes, jnp.int32))

    sizes = jnp.where(number % 4 == 0, named(packed, number // 4), named(usual, number - number // 4 - 1))
    mixed = jax.random.permutation(jax.random.fold_in(own, 3), number_of)
    donor, taker = mixed[0:number_of // 2 * 2:2], mixed[1:number_of // 2 * 2:2]
    margin = jnp.minimum(sizes[donor] - 1, bound - sizes[taker]) // 2
    margin = jnp.where((donor == ranking[0]) | (taker == ranking[0]) | (sizes[taker] == 0), 0, jnp.maximum(margin, 0))
    shifted = jax.random.randint(jax.random.fold_in(own, 4), (number_of // 2,), 0, 1 << 20) % (margin + 1)
    sizes = sizes.at[donor].add(-shifted).at[taker].add(shifted)
    members = jnp.searchsorted(jnp.cumsum(sizes), jnp.arange(rows * top), side="right").astype(jnp.int32)
    grid = members.reshape(top, rows).T
    grid = grid[jax.random.permutation(jax.random.fold_in(own, 1), rows)]
    offset_by = jax.random.randint(jax.random.fold_in(own, 2), (rows, 1), 0, top)
    return jnp.take_along_axis(grid, (jnp.arange(top)[None, :] + offset_by) % top, axis=1)


def portions_of(number_of, total, bound, skew, full):
    loads = [(1 << 20) // math.isqrt(rank ** skew) + 1 for rank in range(1, number_of + 1)]
    largest = bound if full else min(bound, max(-(-total // number_of), total * loads[0] // sum(loads)))
    least = 1 if total - largest >= number_of - 1 else 0
    holding, rest = [largest] + [least] * (number_of - 1), total - largest - least * (number_of - 1)
    while rest > 0:
        candidates = [i for i in range(1, number_of) if holding[i] < largest] or [i for i in range(1, number_of) if holding[i] < bound]
        pool, budget = sum([loads[i] for i in candidates]), rest
        for i in candidates:
            extra = min(bound - holding[i], max(1, budget * loads[i] // pool), rest)
            holding[i] = holding[i] + extra
            rest = rest - extra
    return np.array(holding)


def gaussian(key, extent, width, bound, pieces=(), held_as=jnp.bfloat16):
    loudness = block_levels(key, extent, pieces, -0.22, 0.18) if pieces else 1.0
    array = jax.random.normal(key, extent, jnp.float32) * width * loudness
    return jnp.minimum(jnp.maximum(array, -bound), bound).astype(held_as)


def setup_inputs(seed: int = 0) -> dict:
    splits = jax.random.split(jax.random.key(seed), 8)
    out_grad = gaussian(splits[0], (TOKENS, D), 1.0, 6.0, ((0, 32),))
    hidden = gaussian(splits[1], (TOKENS, TOP, FF), 1.0, 6.0, ((0, 32),))
    expert_ids_keys = jax.random.split(jax.random.fold_in(splits[2], 1), TOKENS // TOK_DEV)
    expert_ids_turns = jax.random.permutation(jax.random.fold_in(splits[2], 3), TOKENS // TOK_DEV)
    expert_ids = jax.vmap(lambda own, number: routed_block(jax.random.fold_in(splits[2], 2), own, number, TOK_DEV, EXPERTS, TOP, CAP, 1))(expert_ids_keys, expert_ids_turns).reshape((TOKENS, TOP))
    gates = jnp.clip(jnp.exp(math.log(0.5) - 3.218876 * jax.random.uniform(splits[3], (TOKENS, TOP), jnp.float32) ** block_levels(splits[3], (TOKENS, TOP), ((0, 32),), -0.2, 0.2)), 0.02, 0.5)
    weights = gaussian(splits[4], (EXPERTS, FF, D), D ** -0.5, 0.125, ((0, 16), (1, 2)))
    row_moment = jnp.clip(jnp.exp(math.log(1024.0) - 4.158883 * jax.random.uniform(splits[5], (EXPERTS, FF), jnp.float32) ** block_levels(splits[5], (EXPERTS, FF), ((0, 16), (1, 2)), -0.2, 0.2)), 16.0, 1024.0)
    col_moment = jnp.clip(jnp.exp(math.log(1024.0) - 4.158883 * jax.random.uniform(splits[6], (EXPERTS, N_REP, D), jnp.float32) ** block_levels(splits[6], (EXPERTS, N_REP, D), ((0, 16), (1, 2)), -0.2, 0.2)), 16.0, 1024.0)
    return dict(out_grad=out_grad, hidden=hidden, expert_ids=expert_ids, gates=gates, weights=weights, row_moment=row_moment, col_moment=col_moment)


decay_rate = 0.9
epsilon = 1e-06

def reference(out_grad, hidden, expert_ids, gates, weights, row_moment, col_moment):
    routes = TOKENS * TOP
    flat_ids = expert_ids.reshape(routes)
    route_index = jnp.arange(routes, dtype=jnp.int32)
    replica_of = route_index // (TOP * TOK_DEV) % N_REP
    flat_hidden = hidden.reshape(routes, FF)
    flat_gates = gates.reshape(routes)
    limit = N_EP * CAP

    def one_expert(expert):
        matrix = weights[expert]
        gradient = jnp.zeros((FF, D), jnp.float32)
        picked = []
        produced = []
        for replica in range(N_REP):
            chosen = (flat_ids == expert) & (replica_of == replica)
            index = jnp.nonzero(chosen, size=limit, fill_value=routes)[0].astype(jnp.int32)
            valid = index < routes
            safe = jnp.minimum(index, routes - 1)
            token = safe // TOP
            factor = jnp.where(valid, flat_gates[safe], jnp.zeros_like(flat_gates[safe]))
            scaled = (factor[:, None] * out_grad[token].astype(jnp.float32)).astype(jnp.bfloat16)
            rows = flat_hidden[safe]
            term = jnp.dot(rows.T, scaled, preferred_element_type=jnp.float32)
            term = lax.optimization_barrier(term.astype(jnp.bfloat16)).astype(jnp.float32)
            gradient = gradient + term
            produced.append(jnp.dot(scaled, matrix.T, preferred_element_type=jnp.float32).astype(jnp.bfloat16))
            picked.append(index)
        return (gradient, jnp.stack(picked), jnp.stack(produced))
    gradients, picked, produced = lax.map(one_expert, jnp.arange(EXPERTS, dtype=jnp.int32))
    hidden_grad = jnp.zeros((routes, FF), jnp.bfloat16).at[picked.reshape(-1)].set(produced.reshape(-1, FF), mode='drop')
    hidden_grad = hidden_grad.reshape(TOKENS, TOP, FF)
    blocks = gradients.reshape(EXPERTS, N_REP, BLK, D)
    squares = blocks * blocks
    row_new = decay_rate * row_moment.reshape(EXPERTS, N_REP, BLK) + (1.0 - decay_rate) * (lax.optimization_barrier(jnp.mean(squares, axis=3)) + epsilon)
    col_new = decay_rate * col_moment + (1.0 - decay_rate) * (lax.optimization_barrier(jnp.mean(squares, axis=2)) + epsilon)
    second = row_new[:, :, :, None] * col_new[:, :, None, :] / lax.optimization_barrier(jnp.mean(row_new, axis=2))[:, :, None, None]
    update = (blocks * lax.rsqrt(second)).astype(jnp.bfloat16).reshape(EXPERTS, FF, D)
    return (hidden_grad, update, row_new.reshape(EXPERTS, FF), col_new)
```

```python
import functools

import jax
import jax.numpy as jnp
from jax import lax
from jax.experimental import pallas as pl
from jax.experimental.pallas import tpu as pltpu
from jax.sharding import PartitionSpec as P

decay_rate = 0.9
epsilon = 1e-06
MESH = pl.DeviceIdType.MESH
scope = jax.named_scope


def up_to(value, step):
    return -(-value // step) * step


def kernel(
    dims,
    og_ref,
    hidden_ref,
    ids_ref,
    gates_ref,
    w_ref,
    rowm_ref,
    colm_ref,
    out_ref,
    update_ref,
    rown_ref,
    coln_ref,
    og_all,
    slot,
    table,
    place_all,
    hsend,
    hrecv,
    rows,
    igbuf,
    back,
    wfull,
    parts,
    grad,
    og_recv,
    own_sem,
    relay_sem,
    y_sem,
    core_sem,
    pl_send,
    pl_recv,
    h_send,
    h_recv,
    r_send,
    r_recv,
    w_send,
    w_recv,
    g_send,
    g_recv,
    l_sem,
):
    n_ep, n_rep, outer, sent, cap, chunks = dims
    tok, width = og_ref.shape
    routes, inner = hidden_ref.shape
    top = routes // tok
    own_rows = inner // n_rep
    wide = width // chunks
    term = wfull
    me = lax.axis_index("ep")
    rep = lax.axis_index("rep")
    z, y, c = me // 4, (me // 2) % 2, me % 2
    y_dev = z * 4 + (1 - y) * 2 + c
    c_dev = z * 4 + y * 2 + (1 - c)
    half = outer // 2
    low = z < half
    near = jnp.where(low, z, outer - 1 - z)
    gateway = near == half - 1

    def real(p):
        return jnp.where(low, p, outer - 1 - p)

    def spot(k):
        return lax.rem(near + k, outer)

    def plane(k):
        return real(spot(k))

    barrier = pltpu.get_barrier_semaphore()
    for d in range(1, n_ep):
        pl.semaphore_signal(
            barrier, inc=1, device_id={"ep": lax.rem(me + d, n_ep)}, device_id_type=MESH
        )
    for d in range(1, n_rep):
        pl.semaphore_signal(
            barrier, inc=1, device_id={"rep": lax.rem(rep + d, n_rep)}, device_id_type=MESH
        )
    with scope("entry"):
        pl.semaphore_wait(barrier, n_ep - 1 + n_rep - 1)

    def remote(src, dst, send, recv, **where):
        return pltpu.make_async_remote_copy(
            src_ref=src, dst_ref=dst, send_sem=send, recv_sem=recv,
            device_id=where, device_id_type=MESH,
        )

    def og_copy(block, send, to, own):
        src = og_ref if own else og_all.at[block]
        return remote(src, og_all.at[block], send, og_recv.at[block], ep=to)

    def og_wait(block):
        remote(og_all.at[block], og_all.at[block], own_sem.at[0], og_recv.at[block], ep=me).wait_recv()

    def column(p):
        return real(p) * 4 + y * 2 + c

    def fan(zs, own, act):
        block = zs * 4 + y * 2 + c
        act(og_copy(block, y_sem.at[zs], y_dev, own))
        act(og_copy(block, core_sem.at[zs * 2], c_dev, own))

    start = lambda copy: copy.start()
    finish = lambda copy: copy.wait_send()

    def own_sends(act):
        for t in range(1, half):
            act(og_copy(me, own_sem.at[t], column(lax.rem(near + t, half)), True))
        fan(z, True, act)

    def own_across(act):
        act(og_copy(me, own_sem.at[0], column(half), True))

    def relay(k, act, arrive):
        block = column(spot(k))
        if arrive:
            og_wait(block)

        @pl.when(gateway & (spot(k) >= half))
        def _():
            for t in range(1, half):
                sem = relay_sem.at[k * half + t]
                act(og_copy(block, sem, column(lax.rem(near + t, half)), False))

        fan(plane(k), False, act)

    def crossing(k, act, arrive):
        zs = plane(k)
        block = zs * 4 + (1 - y) * 2 + c
        if arrive:
            og_wait(block)
        act(og_copy(block, core_sem.at[zs * 2 + 1], c_dev, False))

    own_sends(start)

    @pl.when(gateway)
    def _():
        own_across(start)

    own_og = pltpu.make_async_copy(og_ref, og_all.at[me], l_sem.at[0])
    own_w = pltpu.make_async_copy(w_ref, wfull.at[rep], l_sem.at[1])
    own_hidden = pltpu.make_async_copy(hidden_ref, out_ref, l_sem.at[2])
    own_hidden.start()
    own_og.start()
    own_w.start()
    w_copies = []
    for d in range(1, n_rep):
        q = lax.rem(rep + d, n_rep)
        w_copies.append(remote(w_ref, wfull.at[rep], w_send.at[d], w_recv.at[rep], rep=q))
        w_copies[-1].start()

    experts = lax.broadcasted_iota(jnp.int32, (n_ep, tok), 0)
    chosen = jnp.zeros(experts.shape, jnp.float32)
    gate = jnp.zeros(experts.shape, jnp.float32)
    for k in range(top):
        named = experts == ids_ref[k : k + 1, :]
        chosen = jnp.where(named, 1.0, chosen)
        gate = jnp.where(named, gates_ref[k : k + 1, :], gate)
    row_i = lax.broadcasted_iota(jnp.int32, (tok, tok), 0)
    col_i = lax.broadcasted_iota(jnp.int32, (tok, tok), 1)
    earlier = jnp.where(row_i < col_i, 1.0, 0.0).astype(jnp.bfloat16)
    rank = jnp.dot(chosen.astype(jnp.bfloat16), earlier, preferred_element_type=jnp.float32)
    place = jnp.where(chosen > 0.5, rank, -1.0)
    first_row = lax.broadcasted_iota(jnp.int32, (n_ep, 8, tok), 1) == 0
    table[...] = jnp.where(first_row, place[:, None, :], gate[:, None, :])
    place_all[me] = table[me]
    if cap > sent:
        hrecv[:, sent:, :] = jnp.zeros((n_ep, cap - sent, inner), jnp.bfloat16)
        back[:, sent:, :] = jnp.zeros((n_ep, cap - sent, inner), jnp.bfloat16)

    spread = jnp.where(
        lax.broadcasted_iota(jnp.int32, (tok, routes), 1) // top
        == lax.broadcasted_iota(jnp.int32, (tok, routes), 0), 1.0, 0.0,
    ).astype(jnp.bfloat16)
    named = jnp.dot(
        ids_ref[...].astype(jnp.float32).astype(jnp.bfloat16), spread,
        preferred_element_type=jnp.float32,
    )
    turn = lax.broadcasted_iota(jnp.int32, (top, routes), 1) % top
    mine = turn == lax.broadcasted_iota(jnp.int32, (top, routes), 0)
    named = jnp.sum(jnp.where(mine, named, 0.0), axis=0, keepdims=True)
    ranks = jnp.dot(place.astype(jnp.bfloat16), spread, preferred_element_type=jnp.float32)
    number = lax.broadcasted_iota(jnp.int32, (n_ep, routes), 0).astype(jnp.float32)
    slot[...] = jnp.sum(
        jnp.where(named == number, ranks + number * cap, 0.0), axis=0, keepdims=True
    )

    def place_copy(d):
        e = lax.rem(me + d, n_ep)
        return remote(table.at[e], place_all.at[me], pl_send.at[d], pl_recv.at[me], ep=e)

    @pl.loop(1, n_ep)
    def _(d):
        place_copy(d).start()

    def h_copy(e):
        return remote(hsend.at[e, pl.ds(0, sent)], hrecv.at[me, pl.ds(0, sent)], h_send.at[e], h_recv.at[me], ep=e)

    def r_copy(s):
        return remote(igbuf.at[s, pl.ds(0, sent)], back.at[me, pl.ds(0, sent)], r_send.at[s], r_recv.at[me], ep=s)

    def slot_pick(first):
        ids = lax.broadcasted_iota(jnp.int32, (4 * cap, routes), 0) + first * cap
        return jnp.where(ids.astype(jnp.float32) == slot[...], 1.0, 0.0).astype(jnp.bfloat16)

    def hidden_group(k):
        first = plane(k) * 4
        got = jnp.dot(slot_pick(first), out_ref[...], preferred_element_type=jnp.float32)
        hsend[pl.ds(first, 4)] = got.astype(jnp.bfloat16).reshape(4, cap, inner)
        if k == 0:
            hrecv[me] = hsend[me]

    def hidden_sends(k, ready, lo=0, hi=4):
        first = plane(k) * 4

        @pl.loop(lo, hi)
        def _(i):
            e = first + i

            @pl.when((e != me) & ready)
            def _():
                h_copy(e).start()

    def place_waits():
        @pl.loop(1, n_ep)
        def _(d):
            s = lax.rem(me + d, n_ep)
            remote(table.at[s], place_all.at[s], pl_send.at[d], pl_recv.at[s], ep=s).wait_recv()

    def w_waits():
        for d in range(1, n_rep):
            q = lax.rem(rep + d, n_rep)
            remote(w_ref, wfull.at[q], w_send.at[d], w_recv.at[q], rep=q).wait_recv()

    def held(k):
        return jnp.logical_not(gateway) & (spot(k) >= half)

    def returns(k, straight, free):
        first = plane(k) * 4 + 2 * (y if straight else 1 - y)

        @pl.loop(0, 2)
        def _(i):
            s = first + i

            @pl.when((s != me) & free)
            def _():
                r_copy(s).start()

    def group(k):
        first = plane(k) * 4
        og_wait(first + 1 - c)
        og_wait(first + 3 - c)

        @pl.loop(0, 4)
        def _(i):
            s = first + i
            info = place_all[s]
            ids = lax.broadcasted_iota(jnp.int32, (cap, tok), 0).astype(jnp.float32)
            pick = jnp.where(ids == info[0:1, :], 1.0, 0.0)
            factor = jnp.sum(pick * info[1:2, :], axis=1, keepdims=True)
            got = factor * jnp.dot(
                pick.astype(jnp.bfloat16), og_all[s], preferred_element_type=jnp.float32
            )
            rows[pl.ds(pl.multiple_of(s * cap, 16), cap), :] = got.astype(jnp.bfloat16)

        here = rows[pl.ds(pl.multiple_of(first * cap, 16), 4 * cap), :]
        got = lax.dot_general(
            here,
            wfull[...].reshape(inner, width),
            (((1,), (1,)), ((), ())),
            preferred_element_type=jnp.float32,
        )
        igbuf[pl.ds(first, 4)] = got.astype(jnp.bfloat16).reshape(4, cap, inner)

    with scope("hid_dma"):
        own_hidden.wait()
    last = outer - 1
    turn_k = min(2, last)
    inner_end = jnp.logical_not(gateway)

    def far(k):
        return spot(k) >= half

    def adjacent(k):
        return spot(k) == half

    def early(k):
        return (adjacent(k) & gateway) | (jnp.logical_not(far(k)) & inner_end)

    for k in [*range(1, last), 0, last]:
        with scope(f"hid{k}"):
            hidden_group(k)
        if k == 1:
            hidden_sends(k, early(k), 0, 2)

            @pl.when(inner_end)
            def _():
                own_across(start)

            hidden_sends(k, early(k), 2, 4)
        else:
            hidden_sends(k, k == 0 or early(k))
    for k in range(1, outer):
        with scope(f"relay{k}"):
            relay(k, start, True)
        if k == 1:
            for i in range(1, outer):
                hidden_sends(i, jnp.logical_not(far(i)) & gateway)
            with scope("cross0"):
                crossing(0, start, True)
        if k == turn_k:
            for i in range(1, outer):
                hidden_sends(i, adjacent(i) & inner_end)
    with scope("cross1"):
        crossing(1, start, True)
    with scope("w_wait"):
        place_waits()
        own_og.wait()
        own_w.wait()
        w_waits()
    def beyond(who):
        for k in range(1, outer):
            hidden_sends(k, far(k) & jnp.logical_not(adjacent(k)) & who)

    beyond(inner_end)
    with scope("group0"):
        group(0)
    with scope("group1"):
        group(1)
    beyond(gateway)
    for k in range(2, outer):
        if k == last:
            for i in range(last):
                returns(i, True, jnp.logical_not(held(i)))
        with scope(f"cross{k}"):
            crossing(k, start, True)
        with scope(f"group{k}"):
            group(k)
    returns(last, True, jnp.logical_not(held(last)))

    own = pltpu.make_async_copy(
        igbuf.at[me, pl.ds(0, sent)], back.at[me, pl.ds(0, sent)], r_recv.at[me]
    )
    own.start()

    with scope("h_wait"):
        @pl.loop(1, n_ep)
        def _(d):
            s = lax.rem(me + d, n_ep)
            remote(hsend.at[s, pl.ds(0, sent)], hrecv.at[s, pl.ds(0, sent)], h_send.at[s], h_recv.at[s], ep=s).wait_recv()
    for k in range(1, outer):
        returns(k, True, held(k))

    def g_copy(d, j, q, slot):
        cols = pl.ds(j * wide, wide)
        return remote(
            term.at[q, :, cols], parts.at[slot, :, cols],
            g_send.at[d, j], g_recv.at[slot, j], rep=q,
        )

    left = hrecv[...].reshape(n_ep * cap, inner)
    for j in range(chunks):
        cols = pl.ds(j * wide, wide)
        with scope(f"grad{j}"):
            got = lax.dot_general(
                left, rows[:, cols], (((0,), (0,)), ((), ())), preferred_element_type=jnp.float32
            )
            term[:, :, cols] = got.astype(jnp.bfloat16).reshape(n_rep, own_rows, wide)
        for d in range(1, n_rep):
            g_copy(d, j, lax.rem(rep + d, n_rep), rep).start()

    for k in range(outer):
        returns(k, False, True)

    def collect(j):
        p = lax.rem(near + j, half) if j < half else outer - 1 - (j - half)
        first = real(p) * 4

        with scope(f"rwait{j}"):
            @pl.loop(0, 4)
            def _(i):
                s = first + i

                @pl.when(s != me)
                def _():
                    remote(
                        igbuf.at[s, pl.ds(0, sent)], back.at[s, pl.ds(0, sent)],
                        r_send.at[s], r_recv.at[s], ep=s,
                    ).wait_recv()

        with scope(f"collect{j}"):
            got = lax.dot_general(
                slot_pick(first),
                back[pl.ds(first, 4)].reshape(4 * cap, inner),
                (((0,), (0,)), ((), ())),
                preferred_element_type=jnp.float32,
            ).astype(jnp.bfloat16)
            out_ref[...] = got if j == 0 else out_ref[...] + got

    own.wait()
    for j in range(outer):
        collect(j)

    total = jnp.zeros((own_rows, 1), jnp.float32)
    for j in range(chunks):
        cols = pl.ds(j * wide, wide)
        part = term[rep, :, cols].astype(jnp.float32)
        for d in range(1, n_rep):
            q = lax.rem(rep + d, n_rep)
            with scope(f"gwait{j}"):
                g_copy(d, j, q, q).wait_recv()
            part = part + parts[q, :, cols].astype(jnp.float32)
        grad[:, cols] = part
        square = part * part
        total = total + jnp.sum(square, axis=1, keepdims=True)
        coln_ref[:, cols] = decay_rate * colm_ref[:, cols] + (1.0 - decay_rate) * (
            jnp.sum(square, axis=0, keepdims=True) / own_rows + epsilon
        )
    diagonal = lax.broadcasted_iota(jnp.int32, (own_rows, own_rows), 0) == (
        lax.broadcasted_iota(jnp.int32, (own_rows, own_rows), 1)
    )
    rowm = jnp.sum(jnp.where(diagonal, rowm_ref[...], 0.0), axis=1, keepdims=True)
    row_new = decay_rate * rowm + (1.0 - decay_rate) * (total / width + epsilon)
    rown_ref[...] = jnp.sum(jnp.where(diagonal, row_new, 0.0), axis=0, keepdims=True)
    mean = jnp.sum(row_new, axis=0, keepdims=True) / own_rows
    for j in range(chunks):
        cols = pl.ds(j * wide, wide)
        second = row_new * coln_ref[:, cols] / mean
        with scope(f"update{j}"):
            update_ref[:, cols] = (grad[:, cols] * lax.rsqrt(second)).astype(jnp.bfloat16)

    @pl.loop(1, n_ep)
    def _(d):
        s = lax.rem(me + d, n_ep)
        place_copy(d).wait_send()
        h_copy(s).wait_send()
        r_copy(s).wait_send()

    own_sends(finish)
    own_across(finish)
    crossing(0, finish, False)
    for k in range(1, outer):
        relay(k, finish, False)
        crossing(k, finish, False)
    for copy in w_copies:
        copy.wait_send()
    for j in range(chunks):
        for d in range(1, n_rep):
            g_copy(d, j, lax.rem(rep + d, n_rep), rep).wait_send()


def local(out_grad, hidden, expert_ids, gates, weights, row_moment, col_moment):
    tok, top = expert_ids.shape
    width = out_grad.shape[1]
    inner = hidden.shape[2]
    n_ep, n_rep = lax.axis_size("ep"), lax.axis_size("rep")
    capacity = max(2, tok * top * 9 // (8 * n_ep))
    sent, cap = up_to(capacity, 8), up_to(capacity, 16)
    outer = n_ep // 4
    own_rows = inner // n_rep
    routes = tok * top
    chunks = 4

    vmem = pl.BlockSpec(memory_space=pltpu.VMEM)
    anywhere = pl.BlockSpec(memory_space=pl.ANY)
    dma = pltpu.SemaphoreType.DMA
    hidden_grad, update, row_new, col_new = pl.pallas_call(
        functools.partial(kernel, (n_ep, n_rep, outer, sent, cap, chunks)),
        out_shape=(
            jax.ShapeDtypeStruct((routes, inner), jnp.bfloat16),
            jax.ShapeDtypeStruct((own_rows, width), jnp.bfloat16),
            jax.ShapeDtypeStruct((1, own_rows), jnp.float32),
            jax.ShapeDtypeStruct((1, width), jnp.float32),
        ),
        in_specs=[anywhere, anywhere, vmem, vmem, anywhere, vmem, vmem],
        out_specs=(vmem, vmem, vmem, vmem),
        scratch_shapes=[
            pltpu.VMEM((n_ep, tok, width), jnp.bfloat16),
            pltpu.VMEM((1, routes), jnp.float32),
            pltpu.VMEM((n_ep, 8, tok), jnp.float32),
            pltpu.VMEM((n_ep, 8, tok), jnp.float32),
            pltpu.VMEM((n_ep, cap, inner), jnp.bfloat16),
            pltpu.VMEM((n_ep, cap, inner), jnp.bfloat16),
            pltpu.VMEM((n_ep * cap, width), jnp.bfloat16),
            pltpu.VMEM((n_ep, cap, inner), jnp.bfloat16),
            pltpu.VMEM((n_ep, cap, inner), jnp.bfloat16),
            pltpu.VMEM((n_rep, own_rows, width), jnp.bfloat16),
            pltpu.VMEM((n_rep, own_rows, width), jnp.bfloat16),
            pltpu.VMEM((own_rows, width), jnp.float32),
            dma((n_ep,)),
            dma((outer // 2,)),
            dma((outer * (outer // 2),)),
            dma((outer,)),
            dma((2 * outer,)),
            dma((n_ep,)),
            dma((n_ep,)),
            dma((n_ep,)),
            dma((n_ep,)),
            dma((n_ep,)),
            dma((n_ep,)),
            dma((n_rep,)),
            dma((n_rep,)),
            dma((n_rep, chunks)),
            dma((n_rep, chunks)),
            dma((3,)),
        ],
        compiler_params=pltpu.CompilerParams(
            collective_id=0, has_side_effects=True, vmem_limit_bytes=67043328
        ),
    )(
        out_grad,
        hidden.reshape(routes, inner),
        expert_ids.T,
        gates.T,
        weights[0],
        row_moment.reshape(1, own_rows),
        col_moment.reshape(1, width),
    )

    return (
        hidden_grad.reshape(tok, top, inner),
        update[None],
        row_new.reshape(1, own_rows),
        col_new.reshape(1, 1, width),
    )


def solution(mesh):
    return jax.shard_map(
        local,
        mesh=mesh,
        in_specs=(
            P(("ep", "rep"), None),
            P(("ep", "rep"), None, None),
            P(("ep", "rep"), None),
            P(("ep", "rep"), None),
            P("ep", "rep", None),
            P("ep", "rep"),
            P("ep", "rep", None),
        ),
        out_specs=(
            P(("ep", "rep"), None, None),
            P("ep", "rep", None),
            P("ep", "rep"),
            P("ep", "rep", None),
        ),
        check_vma=False,
    )
```

```python
import functools

import jax
import jax.numpy as jnp
from jax import lax
from jax.experimental import pallas as pl
from jax.experimental.pallas import tpu as pltpu
from jax.sharding import PartitionSpec as P

decay_rate = 0.9
epsilon = 1e-06
MESH = pl.DeviceIdType.MESH
scope = jax.named_scope


def up_to(value, step):
    return -(-value // step) * step


def kernel(
    dims,
    og_ref,
    hidden_ref,
    ids_ref,
    gates_ref,
    w_ref,
    result_ref,
    parts,
    out_ref,
    og_all,
    slot,
    table,
    place_all,
    hsend,
    hrecv,
    rows,
    igbuf,
    back,
    wfull,
    term,
    og_recv,
    own_sem,
    relay_sem,
    y_sem,
    core_sem,
    pl_send,
    pl_recv,
    h_send,
    h_recv,
    r_send,
    r_recv,
    w_send,
    w_recv,
    g_send,
    g_recv,
    l_sem,
):
    n_ep, n_rep, outer, sent, cap, chunks = dims
    tok, width = og_ref.shape
    routes, inner = hidden_ref.shape
    top = routes // tok
    own_rows = inner // n_rep
    wide = width // chunks
    me = lax.axis_index("ep")
    rep = lax.axis_index("rep")
    z, y, c = me // 4, (me // 2) % 2, me % 2
    y_dev = z * 4 + (1 - y) * 2 + c
    c_dev = z * 4 + y * 2 + (1 - c)
    half = outer // 2
    low = z < half
    near = jnp.where(low, z, outer - 1 - z)
    gateway = near == half - 1

    def real(p):
        return jnp.where(low, p, outer - 1 - p)

    def spot(k):
        return lax.rem(near + k, outer)

    def plane(k):
        return real(spot(k))

    barrier = pltpu.get_barrier_semaphore()
    for d in range(1, n_ep):
        pl.semaphore_signal(
            barrier, inc=1, device_id={"ep": lax.rem(me + d, n_ep)}, device_id_type=MESH
        )
    for d in range(1, n_rep):
        pl.semaphore_signal(
            barrier, inc=1, device_id={"rep": lax.rem(rep + d, n_rep)}, device_id_type=MESH
        )
    with scope("entry"):
        pl.semaphore_wait(barrier, n_ep - 1 + n_rep - 1)

    def remote(src, dst, send, recv, **where):
        return pltpu.make_async_remote_copy(
            src_ref=src, dst_ref=dst, send_sem=send, recv_sem=recv,
            device_id=where, device_id_type=MESH,
        )

    def og_copy(block, send, to, own):
        src = og_ref if own else og_all.at[block]
        return remote(src, og_all.at[block], send, og_recv.at[block], ep=to)

    def og_wait(block):
        remote(og_all.at[block], og_all.at[block], own_sem.at[0], og_recv.at[block], ep=me).wait_recv()

    def column(p):
        return real(p) * 4 + y * 2 + c

    def fan(zs, own, act):
        block = zs * 4 + y * 2 + c
        act(og_copy(block, y_sem.at[zs], y_dev, own))
        act(og_copy(block, core_sem.at[zs * 2], c_dev, own))

    start = lambda copy: copy.start()
    finish = lambda copy: copy.wait_send()

    def own_sends(act):
        for t in range(1, half):
            act(og_copy(me, own_sem.at[t], column(lax.rem(near + t, half)), True))
        fan(z, True, act)

    def own_across(act):
        act(og_copy(me, own_sem.at[0], column(half), True))

    def relay(k, act, arrive):
        block = column(spot(k))
        if arrive:
            og_wait(block)

        @pl.when(gateway & (spot(k) >= half))
        def _():
            for t in range(1, half):
                sem = relay_sem.at[k * half + t]
                act(og_copy(block, sem, column(lax.rem(near + t, half)), False))

        fan(plane(k), False, act)

    def crossing(k, act, arrive):
        zs = plane(k)
        block = zs * 4 + (1 - y) * 2 + c
        if arrive:
            og_wait(block)
        act(og_copy(block, core_sem.at[zs * 2 + 1], c_dev, False))

    own_sends(start)

    @pl.when(gateway)
    def _():
        own_across(start)

    own_og = pltpu.make_async_copy(og_ref, og_all.at[me], l_sem.at[0])
    own_w = pltpu.make_async_copy(w_ref, wfull.at[rep], l_sem.at[1])
    own_hidden = pltpu.make_async_copy(hidden_ref, out_ref, l_sem.at[2])
    own_hidden.start()
    own_og.start()
    own_w.start()
    w_copies = []
    for d in range(1, n_rep):
        q = lax.rem(rep + d, n_rep)
        w_copies.append(remote(w_ref, wfull.at[rep], w_send.at[d], w_recv.at[rep], rep=q))
        w_copies[-1].start()

    experts = lax.broadcasted_iota(jnp.int32, (n_ep, tok), 0)
    chosen = jnp.zeros(experts.shape, jnp.float32)
    gate = jnp.zeros(experts.shape, jnp.float32)
    for k in range(top):
        named = experts == ids_ref[k : k + 1, :]
        chosen = jnp.where(named, 1.0, chosen)
        gate = jnp.where(named, gates_ref[k : k + 1, :], gate)
    row_i = lax.broadcasted_iota(jnp.int32, (tok, tok), 0)
    col_i = lax.broadcasted_iota(jnp.int32, (tok, tok), 1)
    earlier = jnp.where(row_i < col_i, 1.0, 0.0).astype(jnp.bfloat16)
    rank = jnp.dot(chosen.astype(jnp.bfloat16), earlier, preferred_element_type=jnp.float32)
    place = jnp.where(chosen > 0.5, rank, -1.0)
    first_row = lax.broadcasted_iota(jnp.int32, (n_ep, 8, tok), 1) == 0
    table[...] = jnp.where(first_row, place[:, None, :], gate[:, None, :])
    place_all[me] = table[me]
    if cap > sent:
        hrecv[:, sent:, :] = jnp.zeros((n_ep, cap - sent, inner), jnp.bfloat16)
        back[:, sent:, :] = jnp.zeros((n_ep, cap - sent, inner), jnp.bfloat16)

    spread = jnp.where(
        lax.broadcasted_iota(jnp.int32, (tok, routes), 1) // top
        == lax.broadcasted_iota(jnp.int32, (tok, routes), 0), 1.0, 0.0,
    ).astype(jnp.bfloat16)
    named = jnp.dot(
        ids_ref[...].astype(jnp.float32).astype(jnp.bfloat16), spread,
        preferred_element_type=jnp.float32,
    )
    turn = lax.broadcasted_iota(jnp.int32, (top, routes), 1) % top
    mine = turn == lax.broadcasted_iota(jnp.int32, (top, routes), 0)
    named = jnp.sum(jnp.where(mine, named, 0.0), axis=0, keepdims=True)
    ranks = jnp.dot(place.astype(jnp.bfloat16), spread, preferred_element_type=jnp.float32)
    number = lax.broadcasted_iota(jnp.int32, (n_ep, routes), 0).astype(jnp.float32)
    slot[...] = jnp.sum(
        jnp.where(named == number, ranks + number * cap, 0.0), axis=0, keepdims=True
    )

    def place_copy(d):
        e = lax.rem(me + d, n_ep)
        return remote(table.at[e], place_all.at[me], pl_send.at[d], pl_recv.at[me], ep=e)

    @pl.loop(1, n_ep)
    def _(d):
        place_copy(d).start()

    def h_copy(e):
        return remote(hsend.at[e, pl.ds(0, sent)], hrecv.at[me, pl.ds(0, sent)], h_send.at[e], h_recv.at[me], ep=e)

    def r_copy(s):
        return remote(igbuf.at[s, pl.ds(0, sent)], back.at[me, pl.ds(0, sent)], r_send.at[s], r_recv.at[me], ep=s)

    def slot_pick(first):
        ids = lax.broadcasted_iota(jnp.int32, (4 * cap, routes), 0) + first * cap
        return jnp.where(ids.astype(jnp.float32) == slot[...], 1.0, 0.0).astype(jnp.bfloat16)

    def hidden_group(k):
        first = plane(k) * 4
        got = jnp.dot(slot_pick(first), out_ref[...], preferred_element_type=jnp.float32)
        hsend[pl.ds(first, 4)] = got.astype(jnp.bfloat16).reshape(4, cap, inner)
        if k == 0:
            hrecv[me] = hsend[me]

    def hidden_sends(k, ready, lo=0, hi=4):
        first = plane(k) * 4

        @pl.loop(lo, hi)
        def _(i):
            e = first + i

            @pl.when((e != me) & ready)
            def _():
                h_copy(e).start()

    def place_waits():
        @pl.loop(1, n_ep)
        def _(d):
            s = lax.rem(me + d, n_ep)
            remote(table.at[s], place_all.at[s], pl_send.at[d], pl_recv.at[s], ep=s).wait_recv()

    def w_waits():
        for d in range(1, n_rep):
            q = lax.rem(rep + d, n_rep)
            remote(w_ref, wfull.at[q], w_send.at[d], w_recv.at[q], rep=q).wait_recv()

    def held(k):
        return jnp.logical_not(gateway) & (spot(k) >= half)

    def returns(k, straight, free):
        first = plane(k) * 4 + 2 * (y if straight else 1 - y)

        @pl.loop(0, 2)
        def _(i):
            s = first + i

            @pl.when((s != me) & free)
            def _():
                r_copy(s).start()

    def gather(k):
        first = plane(k) * 4
        og_wait(first + 1 - c)
        og_wait(first + 3 - c)

        @pl.loop(0, 4)
        def _(i):
            s = first + i
            info = place_all[s]
            ids = lax.broadcasted_iota(jnp.int32, (cap, tok), 0).astype(jnp.float32)
            pick = jnp.where(ids == info[0:1, :], 1.0, 0.0)
            factor = jnp.sum(pick * info[1:2, :], axis=1, keepdims=True)
            got = factor * jnp.dot(
                pick.astype(jnp.bfloat16), og_all[s], preferred_element_type=jnp.float32
            )
            rows[pl.ds(pl.multiple_of(s * cap, 16), cap), :] = got.astype(jnp.bfloat16)

    def product(k):
        first = plane(k) * 4
        here = rows[pl.ds(pl.multiple_of(first * cap, 16), 4 * cap), :]
        got = lax.dot_general(
            here,
            wfull[...].reshape(inner, width),
            (((1,), (1,)), ((), ())),
            preferred_element_type=jnp.float32,
        )
        igbuf[pl.ds(first, 4)] = got.astype(jnp.bfloat16).reshape(4, cap, inner)

    def group(k):
        gather(k)
        product(k)

    with scope("hid_dma"):
        own_hidden.wait()
    last = outer - 1
    turn_k = min(2, last)
    inner_end = jnp.logical_not(gateway)

    def far(k):
        return spot(k) >= half

    def adjacent(k):
        return spot(k) == half

    def early(k):
        return (adjacent(k) & gateway) | (jnp.logical_not(far(k)) & inner_end)

    for k in [*range(1, last), 0, last]:
        with scope(f"hid{k}"):
            hidden_group(k)
        if k == 1:
            hidden_sends(k, early(k), 0, 2)

            @pl.when(inner_end)
            def _():
                own_across(start)

            hidden_sends(k, early(k), 2, 4)
        else:
            hidden_sends(k, k == 0 or early(k))
    for k in range(1, outer):
        with scope(f"relay{k}"):
            relay(k, start, True)
        if k == 1:
            for i in range(1, outer):
                hidden_sends(i, jnp.logical_not(far(i)) & gateway)
            with scope("cross0"):
                crossing(0, start, True)
        if k == turn_k:
            for i in range(1, outer):
                hidden_sends(i, adjacent(i) & inner_end)
    with scope("cross1"):
        crossing(1, start, True)
    with scope("w_wait"):
        place_waits()
        own_og.wait()
        own_w.wait()
        w_waits()
    def beyond(who):
        for k in range(1, outer):
            hidden_sends(k, far(k) & jnp.logical_not(adjacent(k)) & who)

    beyond(inner_end)
    with scope("group0"):
        group(0)
    with scope("group1"):
        group(1)
    beyond(gateway)
    for k in range(2, outer):
        if k == last:
            for i in range(last):
                returns(i, True, jnp.logical_not(held(i)))
        with scope(f"cross{k}"):
            crossing(k, start, True)
        with scope(f"group{k}"):
            if k < last:
                group(k)
            else:
                gather(k)

    with scope("h_wait"):
        @pl.loop(1, n_ep)
        def _(d):
            s = lax.rem(me + d, n_ep)
            remote(hsend.at[s, pl.ds(0, sent)], hrecv.at[s, pl.ds(0, sent)], h_send.at[s], h_recv.at[s], ep=s).wait_recv()
    for k in range(1, last):
        returns(k, True, held(k))
    for k in range(last):
        returns(k, False, True)

    def g_copy(d, j, q, slot):
        cols = pl.ds(j * wide, wide)
        return remote(
            term.at[q, :, cols], parts.at[slot, :, cols],
            g_send.at[d, j], g_recv.at[slot, j], rep=q,
        )

    left = hrecv[...].reshape(n_ep * cap, inner)
    for j in range(chunks):
        cols = pl.ds(j * wide, wide)
        with scope(f"grad{j}"):
            got = lax.dot_general(
                left, rows[:, cols], (((0,), (0,)), ((), ())), preferred_element_type=jnp.float32
            )
            term[:, :, cols] = got.astype(jnp.bfloat16).reshape(n_rep, own_rows, wide)
        for d in range(1, n_rep):
            g_copy(d, j, lax.rem(rep + d, n_rep), rep).start()
        if j == 0:
            with scope("product"):
                product(last)
            returns(last, True, True)
            returns(last, False, True)
            own = pltpu.make_async_copy(
                igbuf.at[me, pl.ds(0, sent)], back.at[me, pl.ds(0, sent)], r_recv.at[me]
            )
            own.start()

    kept = pltpu.make_async_copy(term.at[rep], parts.at[rep], l_sem.at[0])
    kept.start()

    def collect(j):
        p = lax.rem(near + j, half) if j < half else outer - 1 - (j - half)
        first = real(p) * 4

        with scope(f"rwait{j}"):
            @pl.loop(0, 4)
            def _(i):
                s = first + i

                @pl.when(s != me)
                def _():
                    remote(
                        igbuf.at[s, pl.ds(0, sent)], back.at[s, pl.ds(0, sent)],
                        r_send.at[s], r_recv.at[s], ep=s,
                    ).wait_recv()

        with scope(f"collect{j}"):
            got = lax.dot_general(
                slot_pick(first),
                back[pl.ds(first, 4)].reshape(4 * cap, inner),
                (((0,), (0,)), ((), ())),
                preferred_element_type=jnp.float32,
            ).astype(jnp.bfloat16)
            out_ref[...] = got if j == 0 else out_ref[...] + got

    own.wait()
    for j in range(outer):
        collect(j)

    result = pltpu.make_async_copy(out_ref, result_ref, l_sem.at[1])
    result.start()
    @pl.loop(1, n_ep)
    def _(d):
        s = lax.rem(me + d, n_ep)
        place_copy(d).wait_send()
        h_copy(s).wait_send()
        r_copy(s).wait_send()

    own_sends(finish)
    own_across(finish)
    crossing(0, finish, False)
    for k in range(1, outer):
        relay(k, finish, False)
        crossing(k, finish, False)
    for copy in w_copies:
        copy.wait_send()
    for j in range(chunks):
        for d in range(1, n_rep):
            g_copy(d, j, lax.rem(rep + d, n_rep), rep).wait_send()
    kept.wait()
    result.wait()
    for j in range(chunks):
        for d in range(1, n_rep):
            q = lax.rem(rep + d, n_rep)
            with scope(f"gwait{j}"):
                g_copy(d, j, q, q).wait_recv()


def finish_kernel(
    dims,
    result_ref,
    parts_ref,
    rowm_ref,
    colm_ref,
    out_ref,
    update_ref,
    rown_ref,
    coln_ref,
    result,
    parts,
    grad,
    update,
    in_sem,
    part_sem,
    out_sem,
    update_sem,
):
    pieces, chunks = dims
    n_rep, own_rows, width = parts.shape
    wide = width // chunks
    tall = result.shape[0] // pieces

    def load(j):
        cols = pl.ds(j * wide, wide)
        return pltpu.make_async_copy(parts_ref.at[:, :, cols], parts.at[:, :, cols], part_sem.at[j])

    def take(i):
        span = pl.ds(i * tall, tall)
        return pltpu.make_async_copy(result_ref.at[span], result.at[span], in_sem.at[i])

    def give(i):
        span = pl.ds(i * tall, tall)
        return pltpu.make_async_copy(result.at[span], out_ref.at[span], out_sem.at[i])

    def put(j):
        cols = pl.ds(j * wide, wide)
        return pltpu.make_async_copy(update.at[:, cols], update_ref.at[:, cols], update_sem.at[j])

    for j in range(max(chunks, pieces)):
        if j < chunks:
            load(j).start()
        if j < pieces:
            take(j).start()
    diagonal = lax.broadcasted_iota(jnp.int32, (own_rows, own_rows), 0) == (
        lax.broadcasted_iota(jnp.int32, (own_rows, own_rows), 1)
    )
    rowm = jnp.sum(jnp.where(diagonal, rowm_ref[...], 0.0), axis=1, keepdims=True)
    total = jnp.zeros((own_rows, 1), jnp.float32)
    for j in range(chunks):
        cols = pl.ds(j * wide, wide)
        load(j).wait()
        part = parts[0, :, cols].astype(jnp.float32)
        for q in range(1, n_rep):
            part = part + parts[q, :, cols].astype(jnp.float32)
        grad[:, cols] = part
        square = part * part
        total = total + jnp.sum(square, axis=1, keepdims=True)
        coln_ref[:, cols] = decay_rate * colm_ref[:, cols] + (1.0 - decay_rate) * (
            jnp.sum(square, axis=0, keepdims=True) / own_rows + epsilon
        )
        if j < pieces:
            take(j).wait()
            give(j).start()
    for i in range(chunks, pieces):
        take(i).wait()
        give(i).start()
    row_new = decay_rate * rowm + (1.0 - decay_rate) * (total / width + epsilon)
    rown_ref[...] = jnp.sum(jnp.where(diagonal, row_new, 0.0), axis=0, keepdims=True)
    mean = jnp.sum(row_new, axis=0, keepdims=True) / own_rows
    for j in range(chunks):
        cols = pl.ds(j * wide, wide)
        second = row_new * coln_ref[:, cols] / mean
        update[:, cols] = (grad[:, cols] * lax.rsqrt(second)).astype(jnp.bfloat16)
        put(j).start()
    for i in range(pieces):
        give(i).wait()
    for j in range(chunks):
        put(j).wait()


def local(out_grad, hidden, expert_ids, gates, weights, row_moment, col_moment):
    tok, top = expert_ids.shape
    width = out_grad.shape[1]
    inner = hidden.shape[2]
    n_ep, n_rep = lax.axis_size("ep"), lax.axis_size("rep")
    capacity = max(2, tok * top * 9 // (8 * n_ep))
    sent, cap = up_to(capacity, 8), up_to(capacity, 16)
    outer = n_ep // 4
    own_rows = inner // n_rep
    routes = tok * top
    chunks = 4

    vmem = pl.BlockSpec(memory_space=pltpu.VMEM)
    anywhere = pl.BlockSpec(memory_space=pl.ANY)
    dma = pltpu.SemaphoreType.DMA
    result, parts = pl.pallas_call(
        functools.partial(kernel, (n_ep, n_rep, outer, sent, cap, chunks)),
        out_shape=(
            jax.ShapeDtypeStruct((routes, inner), jnp.bfloat16),
            jax.ShapeDtypeStruct((n_rep, own_rows, width), jnp.bfloat16),
        ),
        in_specs=[anywhere, anywhere, vmem, vmem, anywhere],
        out_specs=(anywhere, anywhere),
        scratch_shapes=[
            pltpu.VMEM((routes, inner), jnp.bfloat16),
            pltpu.VMEM((n_ep, tok, width), jnp.bfloat16),
            pltpu.VMEM((1, routes), jnp.float32),
            pltpu.VMEM((n_ep, 8, tok), jnp.float32),
            pltpu.VMEM((n_ep, 8, tok), jnp.float32),
            pltpu.VMEM((n_ep, cap, inner), jnp.bfloat16),
            pltpu.VMEM((n_ep, cap, inner), jnp.bfloat16),
            pltpu.VMEM((n_ep * cap, width), jnp.bfloat16),
            pltpu.VMEM((n_ep, cap, inner), jnp.bfloat16),
            pltpu.VMEM((n_ep, cap, inner), jnp.bfloat16),
            pltpu.VMEM((n_rep, own_rows, width), jnp.bfloat16),
            pltpu.VMEM((n_rep, own_rows, width), jnp.bfloat16),
            dma((n_ep,)),
            dma((outer // 2,)),
            dma((outer * (outer // 2),)),
            dma((outer,)),
            dma((2 * outer,)),
            dma((n_ep,)),
            dma((n_ep,)),
            dma((n_ep,)),
            dma((n_ep,)),
            dma((n_ep,)),
            dma((n_ep,)),
            dma((n_rep,)),
            dma((n_rep,)),
            dma((n_rep, chunks)),
            dma((n_rep, chunks)),
            dma((3,)),
        ],
        compiler_params=pltpu.CompilerParams(
            collective_id=0, has_side_effects=True, vmem_limit_bytes=67043328
        ),
    )(
        out_grad,
        hidden.reshape(routes, inner),
        expert_ids.T,
        gates.T,
        weights[0],
    )
    pieces, blocks = 4, 4
    hidden_grad, update, row_new, col_new = pl.pallas_call(
        functools.partial(finish_kernel, (pieces, blocks)),
        out_shape=(
            jax.ShapeDtypeStruct((routes, inner), jnp.bfloat16),
            jax.ShapeDtypeStruct((own_rows, width), jnp.bfloat16),
            jax.ShapeDtypeStruct((1, own_rows), jnp.float32),
            jax.ShapeDtypeStruct((1, width), jnp.float32),
        ),
        in_specs=[anywhere, anywhere, vmem, vmem],
        out_specs=(anywhere, anywhere, vmem, vmem),
        scratch_shapes=[
            pltpu.VMEM((routes, inner), jnp.bfloat16),
            pltpu.VMEM((n_rep, own_rows, width), jnp.bfloat16),
            pltpu.VMEM((own_rows, width), jnp.float32),
            pltpu.VMEM((own_rows, width), jnp.bfloat16),
            dma((pieces,)),
            dma((blocks,)),
            dma((pieces,)),
            dma((blocks,)),
        ],
        compiler_params=pltpu.CompilerParams(vmem_limit_bytes=67043328),
    )(result, parts, row_moment.reshape(1, own_rows), col_moment.reshape(1, width))

    return (
        hidden_grad.reshape(tok, top, inner),
        update[None],
        row_new.reshape(1, own_rows),
        col_new.reshape(1, 1, width),
    )


def solution(mesh):
    return jax.shard_map(
        local,
        mesh=mesh,
        in_specs=(
            P(("ep", "rep"), None),
            P(("ep", "rep"), None, None),
            P(("ep", "rep"), None),
            P(("ep", "rep"), None),
            P("ep", "rep", None),
            P("ep", "rep"),
            P("ep", "rep", None),
        ),
        out_specs=(
            P(("ep", "rep"), None, None),
            P("ep", "rep", None),
            P("ep", "rep"),
            P("ep", "rep", None),
        ),
        check_vma=False,
    )
```

```python
import functools

import jax
import jax.numpy as jnp
from jax import lax
from jax.experimental import pallas as pl
from jax.experimental.pallas import tpu as pltpu
from jax.sharding import PartitionSpec as P

decay_rate = 0.9
epsilon = 1e-06
MESH = pl.DeviceIdType.MESH
scope = jax.named_scope


def up_to(value, step):
    return -(-value // step) * step


def kernel(
    dims,
    og_ref,
    hidden_ref,
    ids_ref,
    gates_ref,
    w_ref,
    result_ref,
    parts,
    out_ref,
    og_all,
    slot,
    table,
    place_all,
    hsend,
    hrecv,
    rows,
    igbuf,
    back,
    wfull,
    term,
    og_recv,
    own_sem,
    relay_sem,
    y_sem,
    core_sem,
    pl_send,
    pl_recv,
    h_send,
    h_recv,
    r_send,
    r_recv,
    w_send,
    w_recv,
    g_send,
    g_recv,
    l_sem,
    result_sem,
):
    n_ep, n_rep, outer, sent, cap, chunks = dims
    tok, width = og_ref.shape
    routes, inner = hidden_ref.shape
    top = routes // tok
    own_rows = inner // n_rep
    wide = width // chunks
    me = lax.axis_index("ep")
    rep = lax.axis_index("rep")
    z, y, c = me // 4, (me // 2) % 2, me % 2
    y_dev = z * 4 + (1 - y) * 2 + c
    c_dev = z * 4 + y * 2 + (1 - c)
    half = outer // 2
    low = z < half
    near = jnp.where(low, z, outer - 1 - z)
    gateway = near == half - 1

    def real(p):
        return jnp.where(low, p, outer - 1 - p)

    def spot(k):
        return lax.rem(near + k, outer)

    def plane(k):
        return real(spot(k))

    barrier = pltpu.get_barrier_semaphore()
    for d in range(1, n_ep):
        pl.semaphore_signal(
            barrier, inc=1, device_id={"ep": lax.rem(me + d, n_ep)}, device_id_type=MESH
        )
    for d in range(1, n_rep):
        pl.semaphore_signal(
            barrier, inc=1, device_id={"rep": lax.rem(rep + d, n_rep)}, device_id_type=MESH
        )
    with scope("entry"):
        pl.semaphore_wait(barrier, n_ep - 1 + n_rep - 1)

    def remote(src, dst, send, recv, **where):
        return pltpu.make_async_remote_copy(
            src_ref=src, dst_ref=dst, send_sem=send, recv_sem=recv,
            device_id=where, device_id_type=MESH,
        )

    def og_copy(block, send, to, own):
        src = og_ref if own else og_all.at[block]
        return remote(src, og_all.at[block], send, og_recv.at[block], ep=to)

    def og_wait(block):
        remote(og_all.at[block], og_all.at[block], own_sem.at[0], og_recv.at[block], ep=me).wait_recv()

    def column(p):
        return real(p) * 4 + y * 2 + c

    def fan(zs, own, act):
        block = zs * 4 + y * 2 + c
        act(og_copy(block, y_sem.at[zs], y_dev, own))
        act(og_copy(block, core_sem.at[zs * 2], c_dev, own))

    start = lambda copy: copy.start()
    finish = lambda copy: copy.wait_send()

    def own_sends(act):
        for t in range(1, half):
            act(og_copy(me, own_sem.at[t], column(lax.rem(near + t, half)), True))
        fan(z, True, act)

    def own_across(act):
        act(og_copy(me, own_sem.at[0], column(half), True))

    def relay(k, act, arrive):
        block = column(spot(k))
        if arrive:
            og_wait(block)

        @pl.when(gateway & (spot(k) >= half))
        def _():
            for t in range(1, half):
                sem = relay_sem.at[k * half + t]
                act(og_copy(block, sem, column(lax.rem(near + t, half)), False))

        fan(plane(k), False, act)

    def crossing(k, act, arrive):
        zs = plane(k)
        block = zs * 4 + (1 - y) * 2 + c
        if arrive:
            og_wait(block)
        act(og_copy(block, core_sem.at[zs * 2 + 1], c_dev, False))

    own_sends(start)

    @pl.when(gateway)
    def _():
        own_across(start)

    own_og = pltpu.make_async_copy(og_ref, og_all.at[me], l_sem.at[0])
    own_w = pltpu.make_async_copy(w_ref, wfull.at[rep], l_sem.at[1])
    own_hidden = pltpu.make_async_copy(hidden_ref, out_ref, l_sem.at[2])
    own_hidden.start()
    own_og.start()
    own_w.start()
    w_copies = []
    for d in range(1, n_rep):
        q = lax.rem(rep + d, n_rep)
        w_copies.append(remote(w_ref, wfull.at[rep], w_send.at[d], w_recv.at[rep], rep=q))
        w_copies[-1].start()

    experts = lax.broadcasted_iota(jnp.int32, (n_ep, tok), 0)
    chosen = jnp.zeros(experts.shape, jnp.float32)
    gate = jnp.zeros(experts.shape, jnp.float32)
    for k in range(top):
        named = experts == ids_ref[k : k + 1, :]
        chosen = jnp.where(named, 1.0, chosen)
        gate = jnp.where(named, gates_ref[k : k + 1, :], gate)
    row_i = lax.broadcasted_iota(jnp.int32, (tok, tok), 0)
    col_i = lax.broadcasted_iota(jnp.int32, (tok, tok), 1)
    earlier = jnp.where(row_i < col_i, 1.0, 0.0).astype(jnp.bfloat16)
    rank = jnp.dot(chosen.astype(jnp.bfloat16), earlier, preferred_element_type=jnp.float32)
    place = jnp.where(chosen > 0.5, rank, -1.0)
    first_row = lax.broadcasted_iota(jnp.int32, (n_ep, 8, tok), 1) == 0
    table[...] = jnp.where(first_row, place[:, None, :], gate[:, None, :])
    place_all[me] = table[me]
    if cap > sent:
        hrecv[:, sent:, :] = jnp.zeros((n_ep, cap - sent, inner), jnp.bfloat16)
        back[:, sent:, :] = jnp.zeros((n_ep, cap - sent, inner), jnp.bfloat16)

    spread = jnp.where(
        lax.broadcasted_iota(jnp.int32, (tok, routes), 1) // top
        == lax.broadcasted_iota(jnp.int32, (tok, routes), 0), 1.0, 0.0,
    ).astype(jnp.bfloat16)
    named = jnp.dot(
        ids_ref[...].astype(jnp.float32).astype(jnp.bfloat16), spread,
        preferred_element_type=jnp.float32,
    )
    turn = lax.broadcasted_iota(jnp.int32, (top, routes), 1) % top
    mine = turn == lax.broadcasted_iota(jnp.int32, (top, routes), 0)
    named = jnp.sum(jnp.where(mine, named, 0.0), axis=0, keepdims=True)
    ranks = jnp.dot(place.astype(jnp.bfloat16), spread, preferred_element_type=jnp.float32)
    number = lax.broadcasted_iota(jnp.int32, (n_ep, routes), 0).astype(jnp.float32)
    slot[...] = jnp.sum(
        jnp.where(named == number, ranks + number * cap, 0.0), axis=0, keepdims=True
    )

    def place_copy(d):
        e = lax.rem(me + d, n_ep)
        return remote(table.at[e], place_all.at[me], pl_send.at[d], pl_recv.at[me], ep=e)

    @pl.loop(1, n_ep)
    def _(d):
        place_copy(d).start()

    def h_copy(e):
        return remote(hsend.at[e, pl.ds(0, sent)], hrecv.at[me, pl.ds(0, sent)], h_send.at[e], h_recv.at[me], ep=e)

    def r_copy(s):
        return remote(igbuf.at[s, pl.ds(0, sent)], back.at[me, pl.ds(0, sent)], r_send.at[s], r_recv.at[me], ep=s)

    def slot_pick(first):
        ids = lax.broadcasted_iota(jnp.int32, (4 * cap, routes), 0) + first * cap
        return jnp.where(ids.astype(jnp.float32) == slot[...], 1.0, 0.0).astype(jnp.bfloat16)

    def hidden_group(k):
        first = plane(k) * 4
        got = jnp.dot(slot_pick(first), out_ref[...], preferred_element_type=jnp.float32)
        hsend[pl.ds(first, 4)] = got.astype(jnp.bfloat16).reshape(4, cap, inner)
        if k == 0:
            hrecv[me] = hsend[me]

    def hidden_sends(k, ready, lo=0, hi=4):
        first = plane(k) * 4

        @pl.loop(lo, hi)
        def _(i):
            e = first + i

            @pl.when((e != me) & ready)
            def _():
                h_copy(e).start()

    def place_waits():
        @pl.loop(1, n_ep)
        def _(d):
            s = lax.rem(me + d, n_ep)
            remote(table.at[s], place_all.at[s], pl_send.at[d], pl_recv.at[s], ep=s).wait_recv()

    def w_waits():
        for d in range(1, n_rep):
            q = lax.rem(rep + d, n_rep)
            remote(w_ref, wfull.at[q], w_send.at[d], w_recv.at[q], rep=q).wait_recv()

    def held(k):
        return jnp.logical_not(gateway) & (spot(k) >= half)

    def returns(k, straight, free):
        first = plane(k) * 4 + 2 * (y if straight else 1 - y)

        @pl.loop(0, 2)
        def _(i):
            s = first + i

            @pl.when((s != me) & free)
            def _():
                r_copy(s).start()

    def gather(k):
        first = plane(k) * 4
        og_wait(first + 1 - c)
        og_wait(first + 3 - c)

        @pl.loop(0, 4)
        def _(i):
            s = first + i
            info = place_all[s]
            ids = lax.broadcasted_iota(jnp.int32, (cap, tok), 0).astype(jnp.float32)
            pick = jnp.where(ids == info[0:1, :], 1.0, 0.0)
            factor = jnp.sum(pick * info[1:2, :], axis=1, keepdims=True)
            got = factor * jnp.dot(
                pick.astype(jnp.bfloat16), og_all[s], preferred_element_type=jnp.float32
            )
            rows[pl.ds(pl.multiple_of(s * cap, 16), cap), :] = got.astype(jnp.bfloat16)

    def product(k):
        first = plane(k) * 4
        here = rows[pl.ds(pl.multiple_of(first * cap, 16), 4 * cap), :]
        got = lax.dot_general(
            here,
            wfull[...].reshape(inner, width),
            (((1,), (1,)), ((), ())),
            preferred_element_type=jnp.float32,
        )
        igbuf[pl.ds(first, 4)] = got.astype(jnp.bfloat16).reshape(4, cap, inner)

    def group(k):
        gather(k)
        product(k)

    with scope("hid_dma"):
        own_hidden.wait()
    last = outer - 1
    turn_k = min(2, last)
    inner_end = jnp.logical_not(gateway)

    def far(k):
        return spot(k) >= half

    def adjacent(k):
        return spot(k) == half

    def early(k):
        return (adjacent(k) & gateway) | (jnp.logical_not(far(k)) & inner_end)

    for k in [*range(1, last), 0, last]:
        with scope(f"hid{k}"):
            hidden_group(k)
        if k == 1:
            hidden_sends(k, early(k), 0, 2)

            @pl.when(inner_end)
            def _():
                own_across(start)

            hidden_sends(k, early(k), 2, 4)
        else:
            hidden_sends(k, k == 0 or early(k))
    for k in range(1, outer):
        with scope(f"relay{k}"):
            relay(k, start, True)
        if k == 1:
            for i in range(1, outer):
                hidden_sends(i, jnp.logical_not(far(i)) & gateway)
            with scope("cross0"):
                crossing(0, start, True)
        if k == turn_k:
            for i in range(1, outer):
                hidden_sends(i, adjacent(i) & inner_end)
    with scope("cross1"):
        crossing(1, start, True)
    with scope("w_wait"):
        place_waits()
        own_og.wait()
        own_w.wait()
        w_waits()
    def beyond(who):
        for k in range(1, outer):
            hidden_sends(k, far(k) & jnp.logical_not(adjacent(k)) & who)

    beyond(inner_end)
    with scope("group0"):
        group(0)
    with scope("group1"):
        group(1)
    beyond(gateway)
    for k in range(2, outer):
        if k == last:
            for i in range(last):
                returns(i, True, jnp.logical_not(held(i)))
        with scope(f"cross{k}"):
            crossing(k, start, True)
        with scope(f"group{k}"):
            if k < last:
                group(k)
            else:
                gather(k)

    with scope("h_wait"):
        @pl.loop(1, n_ep)
        def _(d):
            s = lax.rem(me + d, n_ep)
            remote(hsend.at[s, pl.ds(0, sent)], hrecv.at[s, pl.ds(0, sent)], h_send.at[s], h_recv.at[s], ep=s).wait_recv()
    for k in range(1, last):
        returns(k, True, held(k))
    for k in range(last):
        returns(k, False, True)

    def g_copy(d, j, q, slot):
        cols = pl.ds(j * wide, wide)
        return remote(
            term.at[q, :, cols], parts.at[slot, :, cols],
            g_send.at[d, j], g_recv.at[slot, j], rep=q,
        )

    left = hrecv[...].reshape(n_ep * cap, inner)
    for j in range(chunks):
        cols = pl.ds(j * wide, wide)
        with scope(f"grad{j}"):
            got = lax.dot_general(
                left, rows[:, cols], (((0,), (0,)), ((), ())), preferred_element_type=jnp.float32
            )
            term[:, :, cols] = got.astype(jnp.bfloat16).reshape(n_rep, own_rows, wide)
        for d in range(1, n_rep):
            g_copy(d, j, lax.rem(rep + d, n_rep), rep).start()
        if j == 0:
            with scope("product"):
                product(last)
            returns(last, True, True)
            returns(last, False, True)
            own = pltpu.make_async_copy(
                igbuf.at[me, pl.ds(0, sent)], back.at[me, pl.ds(0, sent)], r_recv.at[me]
            )
            own.start()

    kept = pltpu.make_async_copy(term.at[rep], parts.at[rep], l_sem.at[0])
    kept.start()

    pieces = 4
    tall = routes // pieces

    def result(i):
        span = pl.ds(i * tall, tall)
        return pltpu.make_async_copy(out_ref.at[span], result_ref.at[span], result_sem.at[i])

    def collect(j):
        p = lax.rem(near + j, half) if j < half else outer - 1 - (j - half)
        first = real(p) * 4

        with scope(f"rwait{j}"):
            @pl.loop(0, 4)
            def _(i):
                s = first + i

                @pl.when(s != me)
                def _():
                    remote(
                        igbuf.at[s, pl.ds(0, sent)], back.at[s, pl.ds(0, sent)],
                        r_send.at[s], r_recv.at[s], ep=s,
                    ).wait_recv()

        if j == last:
            for i in range(pieces):
                span = pl.ds(i * tall, tall)
                ids = lax.broadcasted_iota(jnp.int32, (4 * cap, tall), 0) + first * cap
                pick = jnp.where(ids.astype(jnp.float32) == slot[:, span], 1.0, 0.0)
                got = lax.dot_general(
                    pick.astype(jnp.bfloat16),
                    back[pl.ds(first, 4)].reshape(4 * cap, inner),
                    (((0,), (0,)), ((), ())),
                    preferred_element_type=jnp.float32,
                ).astype(jnp.bfloat16)
                out_ref[span, :] = out_ref[span, :] + got
                result(i).start()
            return

        with scope(f"collect{j}"):
            got = lax.dot_general(
                slot_pick(first),
                back[pl.ds(first, 4)].reshape(4 * cap, inner),
                (((0,), (0,)), ((), ())),
                preferred_element_type=jnp.float32,
            ).astype(jnp.bfloat16)
            out_ref[...] = got if j == 0 else out_ref[...] + got

    own.wait()
    for j in range(outer):
        collect(j)

    @pl.loop(1, n_ep)
    def _(d):
        s = lax.rem(me + d, n_ep)
        place_copy(d).wait_send()
        h_copy(s).wait_send()
        r_copy(s).wait_send()

    own_sends(finish)
    own_across(finish)
    crossing(0, finish, False)
    for k in range(1, outer):
        relay(k, finish, False)
        crossing(k, finish, False)
    for copy in w_copies:
        copy.wait_send()
    for j in range(chunks):
        for d in range(1, n_rep):
            g_copy(d, j, lax.rem(rep + d, n_rep), rep).wait_send()
    kept.wait()
    for i in range(pieces):
        result(i).wait()
    for j in range(chunks):
        for d in range(1, n_rep):
            q = lax.rem(rep + d, n_rep)
            with scope(f"gwait{j}"):
                g_copy(d, j, q, q).wait_recv()


def finish_kernel(
    dims,
    result_ref,
    parts_ref,
    rowm_ref,
    colm_ref,
    out_ref,
    update_ref,
    rown_ref,
    coln_ref,
    result,
    parts,
    grad,
    update,
    in_sem,
    part_sem,
    out_sem,
    update_sem,
):
    pieces, chunks = dims
    n_rep, own_rows, width = parts.shape
    wide = width // chunks
    tall = result.shape[0] // pieces

    def load(j):
        cols = pl.ds(j * wide, wide)
        return pltpu.make_async_copy(parts_ref.at[:, :, cols], parts.at[:, :, cols], part_sem.at[j])

    def take(i):
        span = pl.ds(i * tall, tall)
        return pltpu.make_async_copy(result_ref.at[span], result.at[span], in_sem.at[i])

    def give(i):
        span = pl.ds(i * tall, tall)
        return pltpu.make_async_copy(result.at[span], out_ref.at[span], out_sem.at[i])

    def put(j):
        cols = pl.ds(j * wide, wide)
        return pltpu.make_async_copy(update.at[:, cols], update_ref.at[:, cols], update_sem.at[j])

    for j in range(max(chunks, pieces)):
        if j < chunks:
            load(j).start()
        if j < pieces:
            take(j).start()
    diagonal = lax.broadcasted_iota(jnp.int32, (own_rows, own_rows), 0) == (
        lax.broadcasted_iota(jnp.int32, (own_rows, own_rows), 1)
    )
    rowm = jnp.sum(jnp.where(diagonal, rowm_ref[...], 0.0), axis=1, keepdims=True)
    total = jnp.zeros((own_rows, 1), jnp.float32)
    for j in range(chunks):
        cols = pl.ds(j * wide, wide)
        load(j).wait()
        part = parts[0, :, cols].astype(jnp.float32)
        for q in range(1, n_rep):
            part = part + parts[q, :, cols].astype(jnp.float32)
        grad[:, cols] = part
        square = part * part
        total = total + jnp.sum(square, axis=1, keepdims=True)
        coln_ref[:, cols] = decay_rate * colm_ref[:, cols] + (1.0 - decay_rate) * (
            jnp.sum(square, axis=0, keepdims=True) / own_rows + epsilon
        )
        if j < pieces:
            take(j).wait()
            give(j).start()
    for i in range(chunks, pieces):
        take(i).wait()
        give(i).start()
    row_new = decay_rate * rowm + (1.0 - decay_rate) * (total / width + epsilon)
    rown_ref[...] = jnp.sum(jnp.where(diagonal, row_new, 0.0), axis=0, keepdims=True)
    mean = jnp.sum(row_new, axis=0, keepdims=True) / own_rows
    for j in range(chunks):
        cols = pl.ds(j * wide, wide)
        second = row_new * coln_ref[:, cols] / mean
        update[:, cols] = (grad[:, cols] * lax.rsqrt(second)).astype(jnp.bfloat16)
        put(j).start()
    for i in range(pieces):
        give(i).wait()
    for j in range(chunks):
        put(j).wait()


def local(out_grad, hidden, expert_ids, gates, weights, row_moment, col_moment):
    tok, top = expert_ids.shape
    width = out_grad.shape[1]
    inner = hidden.shape[2]
    n_ep, n_rep = lax.axis_size("ep"), lax.axis_size("rep")
    capacity = max(2, tok * top * 9 // (8 * n_ep))
    sent, cap = up_to(capacity, 8), up_to(capacity, 16)
    outer = n_ep // 4
    own_rows = inner // n_rep
    routes = tok * top
    chunks = 4

    vmem = pl.BlockSpec(memory_space=pltpu.VMEM)
    anywhere = pl.BlockSpec(memory_space=pl.ANY)
    dma = pltpu.SemaphoreType.DMA
    result, parts = pl.pallas_call(
        functools.partial(kernel, (n_ep, n_rep, outer, sent, cap, chunks)),
        out_shape=(
            jax.ShapeDtypeStruct((routes, inner), jnp.bfloat16),
            jax.ShapeDtypeStruct((n_rep, own_rows, width), jnp.bfloat16),
        ),
        in_specs=[anywhere, anywhere, vmem, vmem, anywhere],
        out_specs=(anywhere, anywhere),
        scratch_shapes=[
            pltpu.VMEM((routes, inner), jnp.bfloat16),
            pltpu.VMEM((n_ep, tok, width), jnp.bfloat16),
            pltpu.VMEM((1, routes), jnp.float32),
            pltpu.VMEM((n_ep, 8, tok), jnp.float32),
            pltpu.VMEM((n_ep, 8, tok), jnp.float32),
            pltpu.VMEM((n_ep, cap, inner), jnp.bfloat16),
            pltpu.VMEM((n_ep, cap, inner), jnp.bfloat16),
            pltpu.VMEM((n_ep * cap, width), jnp.bfloat16),
            pltpu.VMEM((n_ep, cap, inner), jnp.bfloat16),
            pltpu.VMEM((n_ep, cap, inner), jnp.bfloat16),
            pltpu.VMEM((n_rep, own_rows, width), jnp.bfloat16),
            pltpu.VMEM((n_rep, own_rows, width), jnp.bfloat16),
            dma((n_ep,)),
            dma((outer // 2,)),
            dma((outer * (outer // 2),)),
            dma((outer,)),
            dma((2 * outer,)),
            dma((n_ep,)),
            dma((n_ep,)),
            dma((n_ep,)),
            dma((n_ep,)),
            dma((n_ep,)),
            dma((n_ep,)),
            dma((n_rep,)),
            dma((n_rep,)),
            dma((n_rep, chunks)),
            dma((n_rep, chunks)),
            dma((3,)),
            dma((4,)),
        ],
        compiler_params=pltpu.CompilerParams(
            collective_id=0, has_side_effects=True, vmem_limit_bytes=67043328
        ),
    )(
        out_grad,
        hidden.reshape(routes, inner),
        expert_ids.T,
        gates.T,
        weights[0],
    )
    pieces, blocks = 4, 4
    hidden_grad, update, row_new, col_new = pl.pallas_call(
        functools.partial(finish_kernel, (pieces, blocks)),
        out_shape=(
            jax.ShapeDtypeStruct((routes, inner), jnp.bfloat16),
            jax.ShapeDtypeStruct((own_rows, width), jnp.bfloat16),
            jax.ShapeDtypeStruct((1, own_rows), jnp.float32),
            jax.ShapeDtypeStruct((1, width), jnp.float32),
        ),
        in_specs=[anywhere, anywhere, vmem, vmem],
        out_specs=(anywhere, anywhere, vmem, vmem),
        scratch_shapes=[
            pltpu.VMEM((routes, inner), jnp.bfloat16),
            pltpu.VMEM((n_rep, own_rows, width), jnp.bfloat16),
            pltpu.VMEM((own_rows, width), jnp.float32),
            pltpu.VMEM((own_rows, width), jnp.bfloat16),
            dma((pieces,)),
            dma((blocks,)),
            dma((pieces,)),
            dma((blocks,)),
        ],
        compiler_params=pltpu.CompilerParams(vmem_limit_bytes=67043328),
    )(result, parts, row_moment.reshape(1, own_rows), col_moment.reshape(1, width))

    return (
        hidden_grad.reshape(tok, top, inner),
        update[None],
        row_new.reshape(1, own_rows),
        col_new.reshape(1, 1, width),
    )


def solution(mesh):
    return jax.shard_map(
        local,
        mesh=mesh,
        in_specs=(
            P(("ep", "rep"), None),
            P(("ep", "rep"), None, None),
            P(("ep", "rep"), None),
            P(("ep", "rep"), None),
            P("ep", "rep", None),
            P("ep", "rep"),
            P("ep", "rep", None),
        ),
        out_specs=(
            P(("ep", "rep"), None, None),
            P("ep", "rep", None),
            P("ep", "rep"),
            P("ep", "rep", None),
        ),
        check_vma=False,
    )
```
